32 devices in a mesh: list: 8 (over y, x, core), shard: 4 (over z).
Axes of the slice: x: 2, y: 2, z: 4, core: 2. Of those that a mesh axis runs over, the one named last changes fastest.
Arguments:
- features: bfloat16 [256, 4096], P(('list', 'shard')), may hold values from -6 to 6
- norm_gain: float32 [4096], replicated, may hold values from 0.5 to 1.5
- gate_weight: bfloat16 [4096, 11008], P('shard', 'list'), may hold values from -0.09375 to 0.09375
- up_weight: bfloat16 [4096, 11008], P('shard', 'list'), may hold values from -0.09375 to 0.09375
- down_weight: bfloat16 [11008, 4096], P('list', 'shard'), may hold values from -0.0546875 to 0.0546875
- centroids: float32 [16, 4096], P('list'), may hold values from -6 to 6
- list_ids: int32 [256], P(('list', 'shard')), may hold values from 0 to 15
- live: int32 [256], P(('list', 'shard')), may hold values 0 or 1
Outputs:
- residuals: bfloat16 [256, 4096], P(('list', 'shard'))
- refreshed: float32 [16, 4096], P('list')
The draws below stay inside these ranges and needn't reach their ends.
All inputs are finite; a program needn't handle non-finite values. No bound on the sum of `live` on one device may be relied on, other than what follows from the above.
Results may differ from the reference program's by a relative error of at most 0.015.
Values may be sent and summed in bfloat16 or wider, within the bound.
A program may use at most 64 MiB of HBM per device.

```python
import math
import jax
import jax.numpy as jnp
import numpy as np
from jax import lax

D = 4096
FF = 11008
PASSAGES = 256
LISTS = 16
N_LIST = 8


def with_ends(drawn, stream_key, low, high):
    shape = drawn.shape
    spot = [jax.random.randint(jax.random.fold_in(stream_key, axis), (), 0, shape[axis]) for axis in range(len(shape))]
    drawn = drawn.at[tuple(spot)].set(low)
    longest = shape.index(max(shape))
    spot[longest] = (spot[longest] + 1) % shape[longest]
    return drawn.at[tuple(spot)].set(high)


def block_levels(rng, extent, shards, smallest, largest):
    loudness = 1.0
    for position, parts in shards:
        heights = jax.random.uniform(jax.random.fold_in(jax.random.fold_in(rng, 6), position), (parts,), jnp.float32, smallest / len(shards), largest / len(shards))
        loudness = loudness * jnp.repeat(jnp.exp(heights), extent[position] // parts).reshape((-1,) + (1,) * (len(extent) - 1 - position))
    return loudness


def rank_bounds(number_of, slope):
    weights = [(1 << 20) // math.isqrt(standing ** slope) + 1 for standing in range(1, number_of + 1)]
    scale = 1 + sum(weights) // (1 << 30)
    return np.cumsum(np.array([max(1, weight // scale) for weight in weights]))


def ranked_ids(rng, shape, amount, skew):
    grid = rank_bounds(amount, skew)
    ticket = jax.random.randint(jax.random.fold_in(rng, 1), shape, 0, int(grid[amount - 1]))
    grade = jnp.searchsorted(jnp.asarray(grid, jnp.int32), ticket, side="right")
    return jax.random.permutation(jax.random.fold_in(rng, 2), amount)[grade].astype(jnp.int32)


def centred(own_key, shape, deviation, limit, split=(), dtype=jnp.bfloat16):
    gain = block_levels(own_key, shape, split, -0.22, 0.18) if split else 1.0
    array = jax.random.normal(own_key, shape, jnp.float32) * deviation * gain
    return jnp.minimum(jnp.maximum(array, -limit), limit).astype(dtype)


def setup_inputs(seed: int = 0) -> dict:
    seeds = jax.random.split(jax.random.key(seed), 9)
    features = centred(seeds[0], (PASSAGES, D), 1.0, 6.0, ((0, 32),))
    norm_gain = jnp.clip(1.0 + 0.1 * jax.random.normal(seeds[1], (D,), jnp.float32), 0.5, 1.5)
    gate_weight = centred(seeds[2], (D, FF), D ** -0.5, 0.09375, ((0, 4), (1, 8)))
    up_weight = centred(seeds[3], (D, FF), D ** -0.5, 0.09375, ((0, 4), (1, 8)))
    down_weight = centred(seeds[4], (FF, D), FF ** -0.5, 0.0546875, ((0, 8), (1, 4)))
    centroids = centred(seeds[5], (LISTS, D), 1.0, 6.0, ((0, 8),), jnp.float32)
    list_ids = with_ends(ranked_ids(seeds[6], (PASSAGES,), LISTS, 2), jax.random.fold_in(seeds[6], 3), 0, LISTS - 1).astype(jnp.int32)
    live = with_ends((jax.random.randint(seeds[7], (PASSAGES,), 0, 8) < 7).astype(jnp.int32), jax.random.fold_in(seeds[7], 1), 0, 1)
    return {"features": features, "norm_gain": norm_gain, "gate_weight": gate_weight, "up_weight": up_weight, "down_weight": down_weight, "centroids": centroids, "list_ids": list_ids, "live": live}


def reference(features, norm_gain, gate_weight, up_weight, down_weight, centroids, list_ids, live):
    gate = jnp.dot(features, gate_weight, preferred_element_type=jnp.float32)
    up_part = jnp.dot(features, up_weight, preferred_element_type=jnp.float32)
    hidden = (jax.nn.silu(gate) * up_part).astype(jnp.bfloat16)
    slice_width = FF // N_LIST
    hidden_parts = hidden.reshape(PASSAGES, N_LIST, slice_width).transpose(1, 0, 2)
    down_parts = down_weight.reshape(N_LIST, slice_width, D)

    def add_term(carry, pair):
        term = jnp.dot(pair[0], pair[1], preferred_element_type=jnp.float32).astype(jnp.bfloat16)
        term = lax.optimization_barrier(term)
        return (carry + term.astype(jnp.float32), None)
    mixed, unused = lax.scan(add_term, jnp.zeros((PASSAGES, D), jnp.float32), (hidden_parts, down_parts))
    stream = features.astype(jnp.float32) + mixed
    scale = lax.rsqrt(lax.optimization_barrier(jnp.mean(stream * stream, axis=1, keepdims=True)) + 1e-05)
    embedding = (stream * scale * norm_gain).astype(jnp.bfloat16)
    rounded = lax.optimization_barrier(centroids.astype(jnp.bfloat16))
    coarse = rounded.astype(jnp.float32)[list_ids]
    alive = live.astype(jnp.float32)
    residuals = (alive[:, None] * (embedding.astype(jnp.float32) - coarse)).astype(jnp.bfloat16)
    sums = jax.ops.segment_sum(embedding.astype(jnp.float32) * alive[:, None], list_ids, num_segments=LISTS)
    counts = jax.ops.segment_sum(alive, list_ids, num_segments=LISTS)
    refreshed = (centroids + sums) / (1.0 + counts[:, None])
    return (residuals, refreshed)
```

```python
import jax
import jax.numpy as jnp
from jax import lax
from jax.sharding import PartitionSpec as P


def body(features, norm_gain, gate_weight, up_weight, down_weight, centroids, list_ids, live):
    width = features.shape[1]
    own_lists = centroids.shape[0]
    column_width = down_weight.shape[1]
    me_list, me_shard = lax.axis_index("list"), lax.axis_index("shard")
    group = lax.all_to_all(features, "shard", split_axis=1, concat_axis=0, tiled=True)
    rows = lax.all_gather(group, "list", axis=0, tiled=True)
    ids_live = lax.all_gather(
        jnp.stack([list_ids, live], axis=1), ("list", "shard"), axis=0, tiled=True
    )
    first = jnp.dot(rows, gate_weight, preferred_element_type=jnp.float32).astype(jnp.bfloat16)
    second = jnp.dot(rows, up_weight, preferred_element_type=jnp.float32).astype(jnp.bfloat16)
    both = lax.psum_scatter(
        jnp.concatenate([first, second], axis=1), "shard", scatter_dimension=0, tiled=True
    ).astype(jnp.float32)
    half = gate_weight.shape[1]
    hidden = (jax.nn.silu(both[:, :half]) * both[:, half:]).astype(jnp.bfloat16)
    hidden = lax.all_gather(hidden, "shard", axis=0, tiled=True)
    terms = jnp.dot(hidden, down_weight, preferred_element_type=jnp.float32)
    part = lax.psum_scatter(
        terms.astype(jnp.bfloat16), "list", scatter_dimension=0, tiled=True
    ).astype(jnp.float32)
    stream = group.astype(jnp.float32) + part
    squares = lax.psum(jnp.sum(stream * stream, axis=1, keepdims=True), "shard")
    scale = lax.rsqrt(squares / width + 1e-05)
    gain = lax.dynamic_slice_in_dim(norm_gain, me_shard * column_width, column_width, 0)
    embedding = (stream * scale * gain).astype(jnp.bfloat16)
    table = lax.all_gather(centroids.astype(jnp.bfloat16), "list", axis=0, tiled=True)
    table = lax.dynamic_slice_in_dim(table, me_shard * column_width, column_width, 1)
    list_total = table.shape[0]
    member = (
        ids_live[:, :1] == jnp.arange(list_total, dtype=jnp.int32)[None, :]
    ).astype(jnp.float32)
    alive = ids_live[:, 1:].astype(jnp.float32)
    weighted = member * alive
    count = lax.dynamic_slice_in_dim(jnp.sum(weighted, axis=0), me_list * own_lists, own_lists, 0)
    group_rows = group.shape[0]
    member = lax.dynamic_slice_in_dim(member, me_list * group_rows, group_rows, 0)
    weighted = lax.dynamic_slice_in_dim(weighted, me_list * group_rows, group_rows, 0)
    alive = lax.dynamic_slice_in_dim(alive, me_list * group_rows, group_rows, 0)
    picked = jnp.dot(member.astype(jnp.bfloat16), table, preferred_element_type=jnp.float32)
    residuals = (alive * (embedding.astype(jnp.float32) - picked)).astype(jnp.bfloat16)
    residuals = lax.all_to_all(residuals, "shard", split_axis=0, concat_axis=1, tiled=True)
    sums = jnp.dot(
        weighted.T.astype(jnp.bfloat16), embedding, preferred_element_type=jnp.float32
    )
    sums = lax.psum_scatter(sums, "list", scatter_dimension=0, tiled=True)
    sums = lax.all_gather(sums, "shard", axis=1, tiled=True)
    refreshed = (centroids + sums) / (1.0 + count[:, None])
    return (residuals, refreshed)


def solution(mesh):
    in_specs = (
        P(("list", "shard"), None),
        P(),
        P("shard", "list"),
        P("shard", "list"),
        P("list", "shard"),
        P("list", None),
        P(("list", "shard")),
        P(("list", "shard")),
    )
    out_specs = (P(("list", "shard"), None), P("list", None))
    return jax.shard_map(body, mesh=mesh, in_specs=in_specs, out_specs=out_specs, check_vma=False)
```

```python
import functools

import jax
import jax.numpy as jnp
from jax import lax
from jax.experimental import pallas as pl
from jax.experimental.pallas import tpu as pltpu
from jax.sharding import PartitionSpec as P

MESH = pl.DeviceIdType.MESH
F32, BF16 = jnp.float32, jnp.bfloat16
FEAT, IDX, GATE, UP, HIDDEN, SQUARES, RESID, FRESH = range(8)
ROWS, IDX2, CENT, TERMS, SUMS = range(5)


def kernel(
    L, S,
    feat, gain, gate, up, down, cents, idx,
    out_res, out_fresh,
    gate_v, up_v, down_v, gain_v, cent_v, idx_v, group_v, rows_v,
    part_send, part_recv, hidden_v, term_send, term_recv, acc_v,
    square_v, res_send, res_recv, sum_send, sum_recv, fresh_v,
    local_sem, ss_sem, sr_sem, ls_sem, lr_sem,
):
    l, s = lax.axis_index("list"), lax.axis_index("shard")
    R, D = feat.shape
    C, G, N = D // S, R * S, R * S * L
    B = N // S
    own = cents.shape[0]
    per = L // S

    def cols(t):
        return pl.ds(pl.multiple_of(t * C, C), C)

    def block(t):
        return pl.ds(pl.multiple_of(t * B, B), B)

    def group(t):
        return pl.ds(pl.multiple_of(t * G, G), G)

    def shard_copy(kind, t, src, dst):
        return pltpu.make_async_remote_copy(
            src_ref=src, dst_ref=dst, send_sem=ss_sem.at[kind, t], recv_sem=sr_sem.at[kind, s],
            device_id={"shard": t}, device_id_type=MESH,
        )

    def shard_recv(kind, t, src, dst):
        pltpu.make_async_remote_copy(
            src_ref=src, dst_ref=dst, send_sem=ss_sem.at[kind, t], recv_sem=sr_sem.at[kind, t],
            device_id={"shard": t}, device_id_type=MESH,
        ).wait_recv()

    def list_copy(kind, t, src, dst):
        return pltpu.make_async_remote_copy(
            src_ref=src, dst_ref=dst, send_sem=ls_sem.at[kind, t], recv_sem=lr_sem.at[kind, l],
            device_id={"list": t}, device_id_type=MESH,
        )

    def list_recv(kind, t, src, dst):
        pltpu.make_async_remote_copy(
            src_ref=src, dst_ref=dst, send_sem=ls_sem.at[kind, t], recv_sem=lr_sem.at[kind, t],
            device_id={"list": t}, device_id_type=MESH,
        ).wait_recv()

    def others(n, me, body):
        @pl.loop(1, n)
        def _(i):
            body(lax.rem(me + i, n))

    locals_ = [
        pltpu.make_async_copy(gate, gate_v, local_sem.at[0]),
        pltpu.make_async_copy(up, up_v, local_sem.at[1]),
        pltpu.make_async_copy(down, down_v, local_sem.at[2]),
        pltpu.make_async_copy(gain.at[:, cols(s)], gain_v, local_sem.at[3]),
        pltpu.make_async_copy(cents.at[:, cols(s)], cent_v.at[l], local_sem.at[4]),
        pltpu.make_async_copy(idx, idx_v.at[l, s], local_sem.at[5]),
        pltpu.make_async_copy(feat.at[:, cols(s)], group_v.at[s], local_sem.at[6]),
    ]
    for copy in (locals_[6], locals_[5], locals_[0], locals_[1], locals_[2], locals_[3], locals_[4]):
        copy.start()

    barrier = pltpu.get_barrier_semaphore()
    others(S, s, lambda t: pl.semaphore_signal(barrier, inc=1, device_id={"shard": t}, device_id_type=MESH))
    others(L, l, lambda t: pl.semaphore_signal(barrier, inc=1, device_id={"list": t}, device_id_type=MESH))
    pl.semaphore_wait(barrier, S + L - 2)

    def send_features(t):
        shard_copy(FEAT, t, feat.at[:, cols(t)], group_v.at[s]).start()
        shard_copy(IDX, t, idx, idx_v.at[l, s]).start()

    others(S, s, send_features)
    others(L, l, lambda t: list_copy(CENT, t, cents.at[:, cols(s)], cent_v.at[l]).start())
    locals_[6].wait()
    locals_[5].wait()

    def recv_features(t):
        shard_recv(FEAT, t, feat.at[:, cols(t)], group_v.at[t])
        shard_recv(IDX, t, idx, idx_v.at[l, t])

    others(S, s, recv_features)
    mine = group_v[...].astype(F32).reshape(G, C)
    acc_v[...] = mine
    rows_v[group(l), :] = mine.astype(BF16)

    def send_rows(t):
        list_copy(ROWS, t, rows_v.at[group(l)], rows_v.at[group(l)]).start()

    others(L, l, send_rows)
    others(L, l, lambda t: list_copy(IDX2, t, idx_v.at[l], idx_v.at[l]).start())
    locals_[0].wait()
    locals_[1].wait()
    others(L, l, lambda t: list_recv(ROWS, t, rows_v.at[group(l)], rows_v.at[group(t)]))

    @pl.loop(1, S + 1)
    def _(i):
        t = lax.rem(s + i, S)
        a = rows_v[block(t), :]
        for kind, weight, k in ((GATE, gate_v, 0), (UP, up_v, 1)):
            part_send[k, t] = jnp.dot(a, weight[...], preferred_element_type=F32).astype(BF16)

            @pl.when(i < S)
            def _():
                shard_copy(kind, t, part_send.at[k, t], part_recv.at[k, s]).start()

    part_recv[0, s] = part_send[0, s]
    part_recv[1, s] = part_send[1, s]

    def recv_parts(t):
        shard_recv(GATE, t, part_send.at[0, t], part_recv.at[0, t])
        shard_recv(UP, t, part_send.at[1, t], part_recv.at[1, t])

    others(S, s, recv_parts)
    first = part_recv[0, 0].astype(F32)
    second = part_recv[1, 0].astype(F32)
    for j in range(1, S):
        first += part_recv[0, j].astype(F32)
        second += part_recv[1, j].astype(F32)
    hidden_v[block(s), :] = (first / (1.0 + jnp.exp(-first)) * second).astype(BF16)
    others(S, s, lambda t: shard_copy(HIDDEN, t, hidden_v.at[block(s)], hidden_v.at[block(s)]).start())

    locals_[2].wait()

    @pl.loop(0, S)
    def _(i):
        t = lax.rem(s + i, S)

        @pl.when(i > 0)
        def _():
            shard_recv(HIDDEN, t, hidden_v.at[block(s)], hidden_v.at[block(t)])

        term_send[block(t), :] = jnp.dot(
            hidden_v[block(t), :], down_v[...], preferred_element_type=F32
        ).astype(BF16)
        for j in range(per):
            g = t * per + j

            @pl.when(g != l)
            def _():
                list_copy(TERMS, g, term_send.at[group(g)], term_recv.at[l]).start()

    acc_v[...] += term_send[group(l), :].astype(F32)

    def add_term(t):
        list_recv(TERMS, t, term_send.at[group(t)], term_recv.at[t])
        acc_v[...] += term_recv[t].astype(F32)

    others(L, l, add_term)
    stream = acc_v[...]
    square_v[s] = jnp.broadcast_to(jnp.sum(stream * stream, axis=1, keepdims=True), (G, 128))
    others(S, s, lambda t: shard_copy(SQUARES, t, square_v.at[s], square_v.at[s]).start())

    for j in (3, 4):
        locals_[j].wait()

    def recv_small(t):
        list_recv(IDX2, t, idx_v.at[l], idx_v.at[t])
        list_recv(CENT, t, cents.at[:, cols(s)], cent_v.at[t])

    others(L, l, recv_small)
    mine_idx = idx_v[l].reshape(G, 256)
    ids, alive = mine_idx[:, :1], mine_idx[:, 128:129].astype(F32)
    coarse = jnp.zeros((G, C), F32)
    for g in range(L):
        for k in range(own):
            row = cent_v[g, k:k + 1, :].astype(BF16).astype(F32)
            coarse = coarse + jnp.where(ids == g * own + k, row, 0.0)
    every = idx_v[...].reshape(N, 256)
    counts = [
        jnp.sum(
            jnp.where(every[:, :128] == l * own + k, every[:, 128:].astype(F32), 0.0),
            axis=0, keepdims=True,
        )[:, :1]
        for k in range(own)
    ]

    others(S, s, lambda t: shard_recv(SQUARES, t, square_v.at[s], square_v.at[t]))
    squares = square_v[0]
    for j in range(1, S):
        squares = squares + square_v[j]
    scale = lax.rsqrt(squares[:, :1] / D + 1e-05)
    embedding = (acc_v[...] * scale * gain_v[...]).astype(BF16).astype(F32)
    weighted = alive * embedding
    for g in range(L):
        for k in range(own):
            sum_send[g, k:k + 1, :] = jnp.sum(
                jnp.where(ids == g * own + k, weighted, 0.0), axis=0, keepdims=True
            )
    others(L, l, lambda t: list_copy(SUMS, t, sum_send.at[t], sum_recv.at[l]).start())
    res_send[...] = (alive * (embedding - coarse)).reshape(S, R, C).astype(BF16)
    others(S, s, lambda t: shard_copy(RESID, t, res_send.at[t], res_recv.at[s]).start())
    res_recv[s] = res_send[s]
    sum_recv[l] = sum_send[l]
    others(L, l, lambda t: list_recv(SUMS, t, sum_send.at[t], sum_recv.at[t]))
    for k in range(own):
        total = cent_v[l, k:k + 1, :]
        for g in range(L):
            total = total + sum_recv[g, k:k + 1, :]
        fresh_v[s, k:k + 1, :] = total / (1.0 + counts[k])
    others(S, s, lambda t: shard_copy(FRESH, t, fresh_v.at[s], fresh_v.at[s]).start())
    others(S, s, lambda t: shard_recv(RESID, t, res_send.at[t], res_recv.at[t]))
    for j in range(S):
        out_res[:, j * C:(j + 1) * C] = res_recv[j]
    others(S, s, lambda t: shard_recv(FRESH, t, fresh_v.at[s], fresh_v.at[t]))
    for j in range(S):
        out_fresh[:, j * C:(j + 1) * C] = fresh_v[j]

    def shard_sent(t):
        shard_copy(FEAT, t, feat.at[:, cols(t)], group_v.at[s]).wait_send()
        shard_copy(IDX, t, idx, idx_v.at[l, s]).wait_send()
        shard_copy(GATE, t, part_send.at[0, t], part_recv.at[0, s]).wait_send()
        shard_copy(UP, t, part_send.at[1, t], part_recv.at[1, s]).wait_send()
        shard_copy(HIDDEN, t, hidden_v.at[block(s)], hidden_v.at[block(s)]).wait_send()
        shard_copy(SQUARES, t, square_v.at[s], square_v.at[s]).wait_send()
        shard_copy(RESID, t, res_send.at[t], res_recv.at[s]).wait_send()
        shard_copy(FRESH, t, fresh_v.at[s], fresh_v.at[s]).wait_send()

    others(S, s, shard_sent)

    def list_sent(t):
        list_copy(ROWS, t, rows_v.at[group(l)], rows_v.at[group(l)]).wait_send()
        list_copy(IDX2, t, idx_v.at[l], idx_v.at[l]).wait_send()
        list_copy(CENT, t, cents.at[:, cols(s)], cent_v.at[l]).wait_send()
        list_copy(TERMS, t, term_send.at[group(t)], term_recv.at[l]).wait_send()
        list_copy(SUMS, t, sum_send.at[t], sum_recv.at[l]).wait_send()

    others(L, l, list_sent)


def solution(mesh):
    L, S = mesh.shape["list"], mesh.shape["shard"]

    def body(features, norm_gain, gate_weight, up_weight, down_weight, centroids, list_ids, live):
        R, D = features.shape
        C, F = gate_weight.shape
        own = centroids.shape[0]
        G, N = R * S, R * S * L
        B = N // S
        packed = jnp.concatenate(
            [jnp.broadcast_to(v[:, None], (R, 128)) for v in (list_ids, live)], axis=1
        )
        return pl.pallas_call(
            functools.partial(kernel, L, S),
            out_shape=(
                jax.ShapeDtypeStruct((R, D), BF16),
                jax.ShapeDtypeStruct((own, D), F32),
            ),
            in_specs=[pl.BlockSpec(memory_space=pl.ANY)] * 7,
            out_specs=[pl.BlockSpec(memory_space=pltpu.VMEM)] * 2,
            scratch_shapes=[
                pltpu.VMEM((C, F), BF16),
                pltpu.VMEM((C, F), BF16),
                pltpu.VMEM((F, C), BF16),
                pltpu.VMEM((1, C), F32),
                pltpu.VMEM((L, own, C), F32),
                pltpu.VMEM((L, S, R, 256), jnp.int32),
                pltpu.VMEM((S, R, C), BF16),
                pltpu.VMEM((N, C), BF16),
                pltpu.VMEM((2, S, B, F), BF16),
                pltpu.VMEM((2, S, B, F), BF16),
                pltpu.VMEM((N, F), BF16),
                pltpu.VMEM((N, C), BF16),
                pltpu.VMEM((L, G, C), BF16),
                pltpu.VMEM((G, C), F32),
                pltpu.VMEM((S, G, 128), F32),
                pltpu.VMEM((S, R, C), BF16),
                pltpu.VMEM((S, R, C), BF16),
                pltpu.VMEM((L, own, C), F32),
                pltpu.VMEM((L, own, C), F32),
                pltpu.VMEM((S, own, C), F32),
                pltpu.SemaphoreType.DMA((7,)),
                pltpu.SemaphoreType.DMA((8, S)),
                pltpu.SemaphoreType.DMA((8, S)),
                pltpu.SemaphoreType.DMA((5, L)),
                pltpu.SemaphoreType.DMA((5, L)),
            ],
            compiler_params=pltpu.CompilerParams(collective_id=0, has_side_effects=True),
        )(features, norm_gain[None, :], gate_weight, up_weight, down_weight, centroids, packed)

    in_specs = (
        P(("list", "shard"), None),
        P(),
        P("shard", "list"),
        P("shard", "list"),
        P("list", "shard"),
        P("list", None),
        P(("list", "shard")),
        P(("list", "shard")),
    )
    out_specs = (P(("list", "shard"), None), P("list", None))
    return jax.shard_map(body, mesh=mesh, in_specs=in_specs, out_specs=out_specs, check_vma=False)
```

```python
import functools

import jax
import jax.numpy as jnp
from jax import lax
from jax.experimental import pallas as pl
from jax.experimental.pallas import tpu as pltpu
from jax.sharding import PartitionSpec as P

MESH = pl.DeviceIdType.MESH
F32, BF16 = jnp.float32, jnp.bfloat16
FEAT, IDX, GATE, UP, HIDDEN, SQUARES, RESID, FRESH = range(8)
ROWS, IDX2, CENT, TERMS, SUMS = range(5)


def kernel(
    L, S,
    feat, gain, gate, up, down, cents, idx,
    out_res, out_fresh,
    gate_v, up_v, down_v, gain_v, cent_v, idx_v, group_v, rows_v,
    part_send, part_recv, hidden_v, term_send, term_recv, acc_v,
    square_v, res_send, res_recv, sum_send, sum_recv, fresh_v,
    local_sem, ss_sem, sr_sem, ls_sem, lr_sem,
):
    l, s = lax.axis_index("list"), lax.axis_index("shard")
    R, D = feat.shape
    C, G, N = D // S, R * S, R * S * L
    B = N // S
    own = cents.shape[0]
    per = L // S

    def cols(t):
        return pl.ds(pl.multiple_of(t * C, C), C)

    def block(t):
        return pl.ds(pl.multiple_of(t * B, B), B)

    def group(t):
        return pl.ds(pl.multiple_of(t * G, G), G)

    def shard_copy(kind, t, src, dst):
        return pltpu.make_async_remote_copy(
            src_ref=src, dst_ref=dst, send_sem=ss_sem.at[kind, t], recv_sem=sr_sem.at[kind, s],
            device_id={"shard": t}, device_id_type=MESH,
        )

    def shard_recv(kind, t, src, dst):
        pltpu.make_async_remote_copy(
            src_ref=src, dst_ref=dst, send_sem=ss_sem.at[kind, t], recv_sem=sr_sem.at[kind, t],
            device_id={"shard": t}, device_id_type=MESH,
        ).wait_recv()

    def list_copy(kind, t, src, dst):
        return pltpu.make_async_remote_copy(
            src_ref=src, dst_ref=dst, send_sem=ls_sem.at[kind, t], recv_sem=lr_sem.at[kind, l],
            device_id={"list": t}, device_id_type=MESH,
        )

    def list_recv(kind, t, src, dst):
        pltpu.make_async_remote_copy(
            src_ref=src, dst_ref=dst, send_sem=ls_sem.at[kind, t], recv_sem=lr_sem.at[kind, t],
            device_id={"list": t}, device_id_type=MESH,
        ).wait_recv()

    def others(n, me, body):
        @pl.loop(1, n)
        def _(i):
            body(lax.rem(me + i, n))

    locals_ = [
        pltpu.make_async_copy(gate, gate_v, local_sem.at[0]),
        pltpu.make_async_copy(up, up_v, local_sem.at[1]),
        pltpu.make_async_copy(down, down_v, local_sem.at[2]),
        pltpu.make_async_copy(gain.at[cols(s)], gain_v.at[0], local_sem.at[3]),
        pltpu.make_async_copy(cents.at[:, cols(s)], cent_v.at[l], local_sem.at[4]),
        pltpu.make_async_copy(idx, idx_v.at[l, s], local_sem.at[5]),
        pltpu.make_async_copy(feat.at[:, cols(s)], group_v.at[s], local_sem.at[6]),
    ]
    for copy in (locals_[6], locals_[5], locals_[0], locals_[1], locals_[2], locals_[3], locals_[4]):
        copy.start()

    barrier = pltpu.get_barrier_semaphore()
    others(S, s, lambda t: pl.semaphore_signal(barrier, inc=1, device_id={"shard": t}, device_id_type=MESH))
    others(L, l, lambda t: pl.semaphore_signal(barrier, inc=1, device_id={"list": t}, device_id_type=MESH))
    pl.semaphore_wait(barrier, S + L - 2)

    def send_features(t):
        shard_copy(FEAT, t, feat.at[:, cols(t)], group_v.at[s]).start()
        shard_copy(IDX, t, idx, idx_v.at[l, s]).start()

    others(S, s, send_features)
    others(L, l, lambda t: list_copy(CENT, t, cents.at[:, cols(s)], cent_v.at[l]).start())
    locals_[6].wait()
    locals_[5].wait()

    def recv_features(t):
        shard_recv(FEAT, t, feat.at[:, cols(t)], group_v.at[t])
        shard_recv(IDX, t, idx, idx_v.at[l, t])

    others(S, s, recv_features)
    mine = group_v[...].astype(F32).reshape(G, C)
    acc_v[...] = mine
    rows_v[group(l), :] = mine.astype(BF16)

    def send_rows(t):
        list_copy(ROWS, t, rows_v.at[group(l)], rows_v.at[group(l)]).start()

    others(L, l, send_rows)
    others(L, l, lambda t: list_copy(IDX2, t, idx_v.at[l], idx_v.at[l]).start())
    locals_[0].wait()
    locals_[1].wait()
    others(L, l, lambda t: list_recv(ROWS, t, rows_v.at[group(l)], rows_v.at[group(t)]))

    @pl.loop(1, S + 1)
    def _(i):
        t = lax.rem(s + i, S)
        a = rows_v[block(t), :]
        for kind, weight, k in ((GATE, gate_v, 0), (UP, up_v, 1)):
            part_send[k, t] = lax.dot_general(
                a, weight[...], (((1,), (1,)), ((), ())), preferred_element_type=F32
            ).astype(BF16)

            @pl.when(i < S)
            def _():
                shard_copy(kind, t, part_send.at[k, t], part_recv.at[k, s]).start()

    part_recv[0, s] = part_send[0, s]
    part_recv[1, s] = part_send[1, s]

    def recv_parts(t):
        shard_recv(GATE, t, part_send.at[0, t], part_recv.at[0, t])
        shard_recv(UP, t, part_send.at[1, t], part_recv.at[1, t])

    others(S, s, recv_parts)
    first = part_recv[0, 0].astype(F32)
    second = part_recv[1, 0].astype(F32)
    for j in range(1, S):
        first += part_recv[0, j].astype(F32)
        second += part_recv[1, j].astype(F32)
    hidden_v[block(s), :] = (first / (1.0 + jnp.exp(-first)) * second).astype(BF16)
    others(S, s, lambda t: shard_copy(HIDDEN, t, hidden_v.at[block(s)], hidden_v.at[block(s)]).start())

    locals_[2].wait()

    @pl.loop(0, S)
    def _(i):
        t = lax.rem(s + i, S)

        @pl.when(i > 0)
        def _():
            shard_recv(HIDDEN, t, hidden_v.at[block(s)], hidden_v.at[block(t)])

        term_send[block(t), :] = jnp.dot(
            hidden_v[block(t), :], down_v[...], preferred_element_type=F32
        ).astype(BF16)
        for j in range(per):
            g = t * per + j

            @pl.when(g != l)
            def _():
                list_copy(TERMS, g, term_send.at[group(g)], term_recv.at[l]).start()

    acc_v[...] += term_send[group(l), :].astype(F32)

    def add_term(t):
        list_recv(TERMS, t, term_send.at[group(t)], term_recv.at[t])
        acc_v[...] += term_recv[t].astype(F32)

    others(L, l, add_term)
    stream = acc_v[...]
    square_v[s] = jnp.broadcast_to(jnp.sum(stream * stream, axis=1, keepdims=True), (G, 128))
    others(S, s, lambda t: shard_copy(SQUARES, t, square_v.at[s], square_v.at[s]).start())

    for j in (3, 4):
        locals_[j].wait()

    def recv_small(t):
        list_recv(IDX2, t, idx_v.at[l], idx_v.at[t])
        list_recv(CENT, t, cents.at[:, cols(s)], cent_v.at[t])

    others(L, l, recv_small)
    mine_idx = idx_v[l].reshape(G, 256)
    ids, alive = mine_idx[:, :1], mine_idx[:, 128:129].astype(F32)
    coarse = jnp.zeros((G, C), F32)
    for g in range(L):
        for k in range(own):
            row = cent_v[g, k:k + 1, :].astype(BF16).astype(F32)
            coarse = coarse + jnp.where(ids == g * own + k, row, 0.0)
    every = idx_v[...].reshape(N, 256)
    counts = [
        jnp.sum(
            jnp.where(every[:, :128] == l * own + k, every[:, 128:].astype(F32), 0.0),
            axis=0, keepdims=True,
        )[:, :1]
        for k in range(own)
    ]

    others(S, s, lambda t: shard_recv(SQUARES, t, square_v.at[s], square_v.at[t]))
    squares = square_v[0]
    for j in range(1, S):
        squares = squares + square_v[j]
    scale = lax.rsqrt(squares[:, :1] / D + 1e-05)
    embedding = (acc_v[...] * scale * gain_v[...]).astype(BF16).astype(F32)
    weighted = alive * embedding
    for g in range(L):
        for k in range(own):
            sum_send[g, k:k + 1, :] = jnp.sum(
                jnp.where(ids == g * own + k, weighted, 0.0), axis=0, keepdims=True
            )
    others(L, l, lambda t: list_copy(SUMS, t, sum_send.at[t], sum_recv.at[l]).start())
    res_send[...] = (alive * (embedding - coarse)).reshape(S, R, C).astype(BF16)
    others(S, s, lambda t: shard_copy(RESID, t, res_send.at[t], res_recv.at[s]).start())
    res_recv[s] = res_send[s]
    sum_recv[l] = sum_send[l]
    others(L, l, lambda t: list_recv(SUMS, t, sum_send.at[t], sum_recv.at[t]))
    for k in range(own):
        total = cent_v[l, k:k + 1, :]
        for g in range(L):
            total = total + sum_recv[g, k:k + 1, :]
        fresh_v[s, k:k + 1, :] = total / (1.0 + counts[k])
    others(S, s, lambda t: shard_copy(FRESH, t, fresh_v.at[s], fresh_v.at[s]).start())
    others(S, s, lambda t: shard_recv(RESID, t, res_send.at[t], res_recv.at[t]))
    for j in range(S):
        out_res[:, j * C:(j + 1) * C] = res_recv[j]
    others(S, s, lambda t: shard_recv(FRESH, t, fresh_v.at[s], fresh_v.at[t]))
    for j in range(S):
        out_fresh[:, j * C:(j + 1) * C] = fresh_v[j]

    def shard_sent(t):
        shard_copy(FEAT, t, feat.at[:, cols(t)], group_v.at[s]).wait_send()
        shard_copy(IDX, t, idx, idx_v.at[l, s]).wait_send()
        shard_copy(GATE, t, part_send.at[0, t], part_recv.at[0, s]).wait_send()
        shard_copy(UP, t, part_send.at[1, t], part_recv.at[1, s]).wait_send()
        shard_copy(HIDDEN, t, hidden_v.at[block(s)], hidden_v.at[block(s)]).wait_send()
        shard_copy(SQUARES, t, square_v.at[s], square_v.at[s]).wait_send()
        shard_copy(RESID, t, res_send.at[t], res_recv.at[s]).wait_send()
        shard_copy(FRESH, t, fresh_v.at[s], fresh_v.at[s]).wait_send()

    others(S, s, shard_sent)

    def list_sent(t):
        list_copy(ROWS, t, rows_v.at[group(l)], rows_v.at[group(l)]).wait_send()
        list_copy(IDX2, t, idx_v.at[l], idx_v.at[l]).wait_send()
        list_copy(CENT, t, cents.at[:, cols(s)], cent_v.at[l]).wait_send()
        list_copy(TERMS, t, term_send.at[group(t)], term_recv.at[l]).wait_send()
        list_copy(SUMS, t, sum_send.at[t], sum_recv.at[l]).wait_send()

    others(L, l, list_sent)


def solution(mesh):
    L, S = mesh.shape["list"], mesh.shape["shard"]

    def body(features, norm_gain, gate_weight, up_weight, down_weight, centroids, list_ids, live):
        R, D = features.shape
        C, F = gate_weight.shape
        own = centroids.shape[0]
        G, N = R * S, R * S * L
        B = N // S
        lane = lax.broadcasted_iota(jnp.int32, (R, 256), 1)
        packed = jnp.where(lane < 128, list_ids[:, None], live[:, None])
        return pl.pallas_call(
            functools.partial(kernel, L, S),
            out_shape=(
                jax.ShapeDtypeStruct((R, D), BF16),
                jax.ShapeDtypeStruct((own, D), F32),
            ),
            in_specs=[pl.BlockSpec(memory_space=pl.ANY)] * 7,
            out_specs=[pl.BlockSpec(memory_space=pltpu.VMEM)] * 2,
            scratch_shapes=[
                pltpu.VMEM((F, C), BF16),
                pltpu.VMEM((F, C), BF16),
                pltpu.VMEM((F, C), BF16),
                pltpu.VMEM((1, C), F32),
                pltpu.VMEM((L, own, C), F32),
                pltpu.VMEM((L, S, R, 256), jnp.int32),
                pltpu.VMEM((S, R, C), BF16),
                pltpu.VMEM((N, C), BF16),
                pltpu.VMEM((2, S, B, F), BF16),
                pltpu.VMEM((2, S, B, F), BF16),
                pltpu.VMEM((N, F), BF16),
                pltpu.VMEM((N, C), BF16),
                pltpu.VMEM((L, G, C), BF16),
                pltpu.VMEM((G, C), F32),
                pltpu.VMEM((S, G, 128), F32),
                pltpu.VMEM((S, R, C), BF16),
                pltpu.VMEM((S, R, C), BF16),
                pltpu.VMEM((L, own, C), F32),
                pltpu.VMEM((L, own, C), F32),
                pltpu.VMEM((S, own, C), F32),
                pltpu.SemaphoreType.DMA((7,)),
                pltpu.SemaphoreType.DMA((8, S)),
                pltpu.SemaphoreType.DMA((8, S)),
                pltpu.SemaphoreType.DMA((5, L)),
                pltpu.SemaphoreType.DMA((5, L)),
            ],
            compiler_params=pltpu.CompilerParams(collective_id=0, has_side_effects=True),
        )(features, norm_gain, gate_weight.T, up_weight.T, down_weight, centroids, packed)

    in_specs = (
        P(("list", "shard"), None),
        P(),
        P("shard", "list"),
        P("shard", "list"),
        P("list", "shard"),
        P("list", None),
        P(("list", "shard")),
        P(("list", "shard")),
    )
    out_specs = (P(("list", "shard"), None), P("list", None))
    return jax.shard_map(body, mesh=mesh, in_specs=in_specs, out_specs=out_specs, check_vma=False)
```

```python
import functools

import jax
import jax.numpy as jnp
from jax import lax
from jax.experimental import pallas as pl
from jax.experimental.pallas import tpu as pltpu
from jax.sharding import PartitionSpec as P

MESH = pl.DeviceIdType.MESH
F32, BF16 = jnp.float32, jnp.bfloat16
FEAT, IDX, SQUARES, RESID, FRESH = range(5)
ROWS, IDX2, CENT, TERMS, SUMS = range(5)


def kernel(
    L, S,
    feat, gain, gate, up, down, cents, idx,
    out_res, out_fresh,
    gate_v, up_v, down_v, gain_v, cent_v, idx_v, group_v, rows_v,
    part_v, part_recv, hidden_v, term_send, term_recv, acc_v,
    square_v, res_send, res_recv, sum_send, sum_recv, fresh_v,
    local_sem, ss_sem, sr_sem, ls_sem, lr_sem, cs_sem, cr_sem, bs_sem, br_sem,
):
    l, s = lax.axis_index("list"), lax.axis_index("shard")
    R, D = feat.shape
    C, G, N = D // S, R * S, R * S * L
    H = N // 2
    K, ck = L, G // 2
    own = cents.shape[0]

    def cols(t):
        return pl.ds(pl.multiple_of(t * C, C), C)

    def group(t):
        return pl.ds(pl.multiple_of(t * G, G), G)

    def shard_copy(kind, t, src, dst):
        return pltpu.make_async_remote_copy(
            src_ref=src, dst_ref=dst, send_sem=ss_sem.at[kind, t], recv_sem=sr_sem.at[kind, s],
            device_id={"shard": t}, device_id_type=MESH,
        )

    def shard_recv(kind, t, src, dst):
        pltpu.make_async_remote_copy(
            src_ref=src, dst_ref=dst, send_sem=ss_sem.at[kind, t], recv_sem=sr_sem.at[kind, t],
            device_id={"shard": t}, device_id_type=MESH,
        ).wait_recv()

    def list_copy(kind, t, src, dst):
        return pltpu.make_async_remote_copy(
            src_ref=src, dst_ref=dst, send_sem=ls_sem.at[kind, t], recv_sem=lr_sem.at[kind, l],
            device_id={"list": t}, device_id_type=MESH,
        )

    def list_recv(kind, t, src, dst):
        pltpu.make_async_remote_copy(
            src_ref=src, dst_ref=dst, send_sem=ls_sem.at[kind, t], recv_sem=lr_sem.at[kind, t],
            device_id={"list": t}, device_id_type=MESH,
        ).wait_recv()

    def others(n, me, body):
        @pl.loop(1, n)
        def _(i):
            body(lax.rem(me + i, n))

    locals_ = [
        pltpu.make_async_copy(gate, gate_v, local_sem.at[0]),
        pltpu.make_async_copy(up, up_v, local_sem.at[1]),
        pltpu.make_async_copy(down, down_v, local_sem.at[2]),
        pltpu.make_async_copy(gain.at[cols(s)], gain_v.at[0], local_sem.at[3]),
        pltpu.make_async_copy(cents.at[:, cols(s)], cent_v.at[l], local_sem.at[4]),
        pltpu.make_async_copy(idx, idx_v.at[l, s], local_sem.at[5]),
        pltpu.make_async_copy(feat.at[:, cols(s)], group_v.at[s], local_sem.at[6]),
    ]
    for copy in (locals_[6], locals_[5], locals_[0], locals_[1], locals_[2], locals_[3], locals_[4]):
        copy.start()

    barrier = pltpu.get_barrier_semaphore()
    others(S, s, lambda t: pl.semaphore_signal(barrier, inc=1, device_id={"shard": t}, device_id_type=MESH))
    others(L, l, lambda t: pl.semaphore_signal(barrier, inc=1, device_id={"list": t}, device_id_type=MESH))
    pl.semaphore_wait(barrier, S + L - 2)

    def send_features(t):
        shard_copy(FEAT, t, feat.at[:, cols(t)], group_v.at[s]).start()
        shard_copy(IDX, t, idx, idx_v.at[l, s]).start()

    others(S, s, send_features)
    others(L, l, lambda t: list_copy(CENT, t, cents.at[:, cols(s)], cent_v.at[l]).start())
    locals_[6].wait()
    locals_[5].wait()

    def recv_features(t):
        shard_recv(FEAT, t, feat.at[:, cols(t)], group_v.at[t])
        shard_recv(IDX, t, idx, idx_v.at[l, t])

    others(S, s, recv_features)
    mine = group_v[...].astype(F32).reshape(G, C)
    acc_v[...] = mine
    rows_v[group(l), :] = mine.astype(BF16)

    def send_rows(t):
        list_copy(ROWS, t, rows_v.at[group(l)], rows_v.at[group(l)]).start()

    others(L, l, send_rows)
    others(L, l, lambda t: list_copy(IDX2, t, idx_v.at[l], idx_v.at[l]).start())
    locals_[0].wait()
    locals_[1].wait()
    others(L, l, lambda t: list_recv(ROWS, t, rows_v.at[group(l)], rows_v.at[group(t)]))

    M = min(H, 4 * G)

    def chain_copy(h, k, t):
        return pltpu.make_async_remote_copy(
            src_ref=part_v.at[h, k], dst_ref=part_recv.at[h, k],
            send_sem=cs_sem.at[h, k], recv_sem=cr_sem.at[h, k],
            device_id={"shard": t}, device_id_type=MESH,
        )

    def chunk(h, k):
        return pl.ds(pl.multiple_of((h * K + k) * ck, ck), ck)

    def back_copy(h, k, t):
        return pltpu.make_async_remote_copy(
            src_ref=hidden_v.at[chunk(h, k)], dst_ref=hidden_v.at[chunk(h, k)],
            send_sem=bs_sem.at[h, k], recv_sem=br_sem.at[h, k],
            device_id={"shard": t}, device_id_type=MESH,
        )

    def place(h):
        return h * s + (1 - h) * (S - 1 - s), s + (2 * h - 1), s - (2 * h - 1)

    early = 1 - s // max(S // 2, 1)

    @pl.loop(0, 2)
    def _(i):
        h = lax.rem(early + i, 2)
        p, nxt, prv = place(h)

        @pl.loop(0, H // M)
        def _(b):
            a = rows_v[pl.ds(pl.multiple_of(h * H + b * M, M), M), :]
            for j, weight in ((0, gate_v), (1, up_v)):
                product = lax.dot_general(
                    a, weight[...], (((1,), (1,)), ((), ())), preferred_element_type=F32
                ).astype(BF16)
                for c in range(M // ck):
                    part_v[h, b * (M // ck) + c, j] = product[c * ck:(c + 1) * ck, :]

        @pl.when(p == 0)
        def _():
            @pl.loop(0, K)
            def _(k):
                chain_copy(h, k, nxt).start()

    locals_[2].wait()

    def finish(h, k):
        @pl.when(lax.rem(k, 2) == 1)
        def _():
            g = h * (L // 2) + k // 2
            term_send[group(g), :] = jnp.dot(
                hidden_v[group(g), :], down_v[...], preferred_element_type=F32
            ).astype(BF16)

            @pl.when(g != l)
            def _():
                list_copy(TERMS, g, term_send.at[group(g)], term_recv.at[l]).start()

    @pl.loop(0, 6 * (S - 1) + K)
    def _(step):
        @pl.loop(0, 2)
        def _(h):
            p, nxt, prv = place(h)
            k = step - 3 * p

            @pl.when((p > 0) & (k >= 0) & (k < K))
            def _():
                chain_copy(h, k, prv).wait_recv()

                @pl.when(p < S - 1)
                def _():
                    part_v[h, k] = (part_v[h, k].astype(F32) + part_recv[h, k].astype(F32)).astype(BF16)
                    chain_copy(h, k, nxt).start()

                @pl.when(p == S - 1)
                def _():
                    first = part_v[h, k, 0].astype(F32) + part_recv[h, k, 0].astype(F32)
                    second = part_v[h, k, 1].astype(F32) + part_recv[h, k, 1].astype(F32)
                    hidden_v[chunk(h, k), :] = (first / (1.0 + jnp.exp(-first)) * second).astype(BF16)
                    back_copy(h, k, prv).start()
                    finish(h, k)

            q = step - 3 * (S - 1) - 3 * (S - 1 - p)

            @pl.when((p < S - 1) & (q >= 0) & (q < K))
            def _():
                back_copy(h, q, nxt).wait_recv()

                @pl.when(p > 0)
                def _():
                    back_copy(h, q, prv).start()

                finish(h, q)

    acc_v[...] += term_send[group(l), :].astype(F32)

    def add_term(t):
        list_recv(TERMS, t, term_send.at[group(t)], term_recv.at[t])
        acc_v[...] += term_recv[t].astype(F32)

    others(L, l, add_term)
    stream = acc_v[...]
    square_v[s] = jnp.broadcast_to(jnp.sum(stream * stream, axis=1, keepdims=True), (G, 128))
    others(S, s, lambda t: shard_copy(SQUARES, t, square_v.at[s], square_v.at[s]).start())

    for j in (3, 4):
        locals_[j].wait()

    def recv_small(t):
        list_recv(IDX2, t, idx_v.at[l], idx_v.at[t])
        list_recv(CENT, t, cents.at[:, cols(s)], cent_v.at[t])

    others(L, l, recv_small)
    mine_idx = idx_v[l].reshape(G, 256)
    ids, alive = mine_idx[:, :1], mine_idx[:, 128:129].astype(F32)
    coarse = jnp.zeros((G, C), F32)
    for g in range(L):
        for k in range(own):
            row = cent_v[g, k:k + 1, :].astype(BF16).astype(F32)
            coarse = coarse + jnp.where(ids == g * own + k, row, 0.0)
    every = idx_v[...].reshape(N, 256)
    counts = [
        jnp.sum(
            jnp.where(every[:, :128] == l * own + k, every[:, 128:].astype(F32), 0.0),
            axis=0, keepdims=True,
        )[:, :1]
        for k in range(own)
    ]

    others(S, s, lambda t: shard_recv(SQUARES, t, square_v.at[s], square_v.at[t]))
    squares = square_v[0]
    for j in range(1, S):
        squares = squares + square_v[j]
    scale = lax.rsqrt(squares[:, :1] / D + 1e-05)
    embedding = (acc_v[...] * scale * gain_v[...]).astype(BF16).astype(F32)
    weighted = alive * embedding
    for g in range(L):
        for k in range(own):
            sum_send[g, k:k + 1, :] = jnp.sum(
                jnp.where(ids == g * own + k, weighted, 0.0), axis=0, keepdims=True
            )
    others(L, l, lambda t: list_copy(SUMS, t, sum_send.at[t], sum_recv.at[l]).start())
    res_send[...] = (alive * (embedding - coarse)).reshape(S, R, C).astype(BF16)
    others(S, s, lambda t: shard_copy(RESID, t, res_send.at[t], res_recv.at[s]).start())
    res_recv[s] = res_send[s]
    sum_recv[l] = sum_send[l]
    others(L, l, lambda t: list_recv(SUMS, t, sum_send.at[t], sum_recv.at[t]))
    for k in range(own):
        total = cent_v[l, k:k + 1, :]
        for g in range(L):
            total = total + sum_recv[g, k:k + 1, :]
        fresh_v[s, k:k + 1, :] = total / (1.0 + counts[k])
    others(S, s, lambda t: shard_copy(FRESH, t, fresh_v.at[s], fresh_v.at[s]).start())
    others(S, s, lambda t: shard_recv(RESID, t, res_send.at[t], res_recv.at[t]))
    for j in range(S):
        out_res[:, j * C:(j + 1) * C] = res_recv[j]
    others(S, s, lambda t: shard_recv(FRESH, t, fresh_v.at[s], fresh_v.at[t]))
    for j in range(S):
        out_fresh[:, j * C:(j + 1) * C] = fresh_v[j]

    def shard_sent(t):
        shard_copy(FEAT, t, feat.at[:, cols(t)], group_v.at[s]).wait_send()
        shard_copy(IDX, t, idx, idx_v.at[l, s]).wait_send()
        shard_copy(SQUARES, t, square_v.at[s], square_v.at[s]).wait_send()
        shard_copy(RESID, t, res_send.at[t], res_recv.at[s]).wait_send()
        shard_copy(FRESH, t, fresh_v.at[s], fresh_v.at[s]).wait_send()

    others(S, s, shard_sent)

    def list_sent(t):
        list_copy(ROWS, t, rows_v.at[group(l)], rows_v.at[group(l)]).wait_send()
        list_copy(IDX2, t, idx_v.at[l], idx_v.at[l]).wait_send()
        list_copy(CENT, t, cents.at[:, cols(s)], cent_v.at[l]).wait_send()
        list_copy(TERMS, t, term_send.at[group(t)], term_recv.at[l]).wait_send()
        list_copy(SUMS, t, sum_send.at[t], sum_recv.at[l]).wait_send()

    others(L, l, list_sent)

    @pl.loop(0, 2)
    def _(h):
        p, nxt, prv = place(h)

        @pl.loop(0, K)
        def _(k):
            @pl.when(p < S - 1)
            def _():
                chain_copy(h, k, nxt).wait_send()

            @pl.when(p > 0)
            def _():
                back_copy(h, k, prv).wait_send()


def solution(mesh):
    L, S = mesh.shape["list"], mesh.shape["shard"]

    def body(features, norm_gain, gate_weight, up_weight, down_weight, centroids, list_ids, live):
        R, D = features.shape
        C, F = gate_weight.shape
        own = centroids.shape[0]
        G, N = R * S, R * S * L
        lane = lax.broadcasted_iota(jnp.int32, (R, 256), 1)
        packed = jnp.where(lane < 128, list_ids[:, None], live[:, None])
        return pl.pallas_call(
            functools.partial(kernel, L, S),
            out_shape=(
                jax.ShapeDtypeStruct((R, D), BF16),
                jax.ShapeDtypeStruct((own, D), F32),
            ),
            in_specs=[pl.BlockSpec(memory_space=pl.ANY)] * 7,
            out_specs=[pl.BlockSpec(memory_space=pltpu.VMEM)] * 2,
            scratch_shapes=[
                pltpu.VMEM((F, C), BF16),
                pltpu.VMEM((F, C), BF16),
                pltpu.VMEM((F, C), BF16),
                pltpu.VMEM((1, C), F32),
                pltpu.VMEM((L, own, C), F32),
                pltpu.VMEM((L, S, R, 256), jnp.int32),
                pltpu.VMEM((S, R, C), BF16),
                pltpu.VMEM((N, C), BF16),
                pltpu.VMEM((2, L, 2, G // 2, F), BF16),
                pltpu.VMEM((2, L, 2, G // 2, F), BF16),
                pltpu.VMEM((N, F), BF16),
                pltpu.VMEM((N, C), BF16),
                pltpu.VMEM((L, G, C), BF16),
                pltpu.VMEM((G, C), F32),
                pltpu.VMEM((S, G, 128), F32),
                pltpu.VMEM((S, R, C), BF16),
                pltpu.VMEM((S, R, C), BF16),
                pltpu.VMEM((L, own, C), F32),
                pltpu.VMEM((L, own, C), F32),
                pltpu.VMEM((S, own, C), F32),
                pltpu.SemaphoreType.DMA((7,)),
                pltpu.SemaphoreType.DMA((5, S)),
                pltpu.SemaphoreType.DMA((5, S)),
                pltpu.SemaphoreType.DMA((5, L)),
                pltpu.SemaphoreType.DMA((5, L)),
                pltpu.SemaphoreType.DMA((2, L)),
                pltpu.SemaphoreType.DMA((2, L)),
                pltpu.SemaphoreType.DMA((2, L)),
                pltpu.SemaphoreType.DMA((2, L)),
            ],
            compiler_params=pltpu.CompilerParams(collective_id=0, has_side_effects=True),
        )(features, norm_gain, gate_weight.T, up_weight.T, down_weight, centroids, packed)

    in_specs = (
        P(("list", "shard"), None),
        P(),
        P("shard", "list"),
        P("shard", "list"),
        P("list", "shard"),
        P("list", None),
        P(("list", "shard")),
        P(("list", "shard")),
    )
    out_specs = (P(("list", "shard"), None), P("list", None))
    return jax.shard_map(body, mesh=mesh, in_specs=in_specs, out_specs=out_specs, check_vma=False)
```

```python
import functools

import jax
import jax.numpy as jnp
from jax import lax
from jax.experimental import pallas as pl
from jax.experimental.pallas import tpu as pltpu
from jax.sharding import PartitionSpec as P

MESH = pl.DeviceIdType.MESH
F32, BF16 = jnp.float32, jnp.bfloat16
FEAT, IDX, SQUARES, RESID, FRESH = range(5)
ROWS, IDX2, CENT, TERMS, SUMS, PASSED = range(6)


def kernel(
    L, S,
    feat, gain, gate, up, down, cents, idx,
    out_res, out_fresh,
    gate_v, up_v, down_v, gain_v, cent_v, idx_v, group_v, rows_v,
    part_v, part_recv, hidden_v, term_send, term_recv, acc_v,
    square_v, res_send, res_recv, sum_send, sum_recv, fresh_v,
    local_sem, ss_sem, sr_sem, ls_sem, lr_sem, cs_sem, cr_sem, bs_sem, br_sem,
):
    l, s = lax.axis_index("list"), lax.axis_index("shard")
    R, D = feat.shape
    C, G, N = D // S, R * S, R * S * L
    H = N // 2
    K, ck = L, G // 2
    own = cents.shape[0]

    def cols(t):
        return pl.ds(pl.multiple_of(t * C, C), C)

    def group(t):
        return pl.ds(pl.multiple_of(t * G, G), G)

    def shard_copy(kind, t, src, dst):
        return pltpu.make_async_remote_copy(
            src_ref=src, dst_ref=dst, send_sem=ss_sem.at[kind, t], recv_sem=sr_sem.at[kind, s],
            device_id={"shard": t}, device_id_type=MESH,
        )

    def shard_recv(kind, t, src, dst):
        pltpu.make_async_remote_copy(
            src_ref=src, dst_ref=dst, send_sem=ss_sem.at[kind, t], recv_sem=sr_sem.at[kind, t],
            device_id={"shard": t}, device_id_type=MESH,
        ).wait_recv()

    def list_copy(kind, t, src, dst):
        return pltpu.make_async_remote_copy(
            src_ref=src, dst_ref=dst, send_sem=ls_sem.at[kind, t], recv_sem=lr_sem.at[kind, l],
            device_id={"list": t}, device_id_type=MESH,
        )

    def list_recv(kind, t, src, dst):
        pltpu.make_async_remote_copy(
            src_ref=src, dst_ref=dst, send_sem=ls_sem.at[kind, t], recv_sem=lr_sem.at[kind, t],
            device_id={"list": t}, device_id_type=MESH,
        ).wait_recv()

    def others(n, me, body):
        @pl.loop(1, n)
        def _(i):
            body(lax.rem(me + i, n))

    locals_ = [
        pltpu.make_async_copy(gate, gate_v, local_sem.at[0]),
        pltpu.make_async_copy(up, up_v, local_sem.at[1]),
        pltpu.make_async_copy(down, down_v, local_sem.at[2]),
        pltpu.make_async_copy(gain.at[cols(s)], gain_v.at[0], local_sem.at[3]),
        pltpu.make_async_copy(cents.at[:, cols(s)], cent_v.at[l], local_sem.at[4]),
        pltpu.make_async_copy(idx, idx_v.at[l, s], local_sem.at[5]),
        pltpu.make_async_copy(feat.at[:, cols(s)], group_v.at[s], local_sem.at[6]),
    ]
    for copy in (locals_[6], locals_[5], locals_[0], locals_[1], locals_[2], locals_[3], locals_[4]):
        copy.start()

    barrier = pltpu.get_barrier_semaphore()
    others(S, s, lambda t: pl.semaphore_signal(barrier, inc=1, device_id={"shard": t}, device_id_type=MESH))
    others(L, l, lambda t: pl.semaphore_signal(barrier, inc=1, device_id={"list": t}, device_id_type=MESH))
    pl.semaphore_wait(barrier, S + L - 2)

    def send_features(t):
        shard_copy(FEAT, t, feat.at[:, cols(t)], group_v.at[s]).start()
        shard_copy(IDX, t, idx, idx_v.at[l, s]).start()

    others(S, s, send_features)
    others(L, l, lambda t: list_copy(CENT, t, cents.at[:, cols(s)], cent_v.at[l]).start())
    locals_[6].wait()
    locals_[5].wait()

    def recv_features(t):
        shard_recv(FEAT, t, feat.at[:, cols(t)], group_v.at[t])
        shard_recv(IDX, t, idx, idx_v.at[l, t])

    others(S, s, recv_features)
    mine = group_v[...].astype(F32).reshape(G, C)
    acc_v[...] = mine
    rows_v[group(l), :] = mine.astype(BF16)

    def send_rows(t):
        list_copy(ROWS, t, rows_v.at[group(l)], rows_v.at[group(l)]).start()

    mate = l + 1 - 2 * lax.rem(l, 2)

    def peers(me, body):
        @pl.loop(1, L // 2)
        def _(i):
            body(lax.rem(me + 2 * i, L))

    peers(l, send_rows)
    send_rows(mate)
    others(L, l, lambda t: list_copy(IDX2, t, idx_v.at[l], idx_v.at[l]).start())
    locals_[0].wait()
    locals_[1].wait()

    def pass_on(t):
        return pltpu.make_async_remote_copy(
            src_ref=rows_v.at[group(t)], dst_ref=rows_v.at[group(t)],
            send_sem=ls_sem.at[PASSED, t], recv_sem=lr_sem.at[PASSED, t],
            device_id={"list": mate}, device_id_type=MESH,
        )

    def relay_rows(t):
        list_recv(ROWS, t, rows_v.at[group(l)], rows_v.at[group(t)])
        pass_on(t).start()

    peers(l, relay_rows)
    list_recv(ROWS, mate, rows_v.at[group(l)], rows_v.at[group(mate)])
    peers(mate, lambda t: pass_on(t).wait_recv())

    M = min(H, 4 * G)

    def chain_copy(h, k, t):
        return pltpu.make_async_remote_copy(
            src_ref=part_v.at[h, k], dst_ref=part_recv.at[h, k],
            send_sem=cs_sem.at[h, k], recv_sem=cr_sem.at[h, k],
            device_id={"shard": t}, device_id_type=MESH,
        )

    def chunk(h, k):
        return pl.ds(pl.multiple_of((h * K + k) * ck, ck), ck)

    def back_copy(h, k, t):
        return pltpu.make_async_remote_copy(
            src_ref=hidden_v.at[chunk(h, k)], dst_ref=hidden_v.at[chunk(h, k)],
            send_sem=bs_sem.at[h, k], recv_sem=br_sem.at[h, k],
            device_id={"shard": t}, device_id_type=MESH,
        )

    def place(h):
        return h * s + (1 - h) * (S - 1 - s), s + (2 * h - 1), s - (2 * h - 1)

    early = 1 - s // max(S // 2, 1)

    @pl.loop(0, 2)
    def _(i):
        h = lax.rem(early + i, 2)
        p, nxt, prv = place(h)

        @pl.loop(0, H // M)
        def _(b):
            a = rows_v[pl.ds(pl.multiple_of(h * H + b * M, M), M), :]
            for j, weight in ((0, gate_v), (1, up_v)):
                product = lax.dot_general(
                    a, weight[...], (((1,), (1,)), ((), ())), preferred_element_type=F32
                ).astype(BF16)
                for c in range(M // ck):
                    part_v[h, b * (M // ck) + c, j] = product[c * ck:(c + 1) * ck, :]

        @pl.when(p == 0)
        def _():
            @pl.loop(0, K)
            def _(k):
                chain_copy(h, k, nxt).start()

    locals_[2].wait()

    def finish(h, k):
        @pl.when(lax.rem(k, 2) == 1)
        def _():
            g = h * (L // 2) + k // 2
            term_send[group(g), :] = jnp.dot(
                hidden_v[group(g), :], down_v[...], preferred_element_type=F32
            ).astype(BF16)

            @pl.when(g != l)
            def _():
                list_copy(TERMS, g, term_send.at[group(g)], term_recv.at[l]).start()

    @pl.loop(0, 6 * (S - 1) + K)
    def _(step):
        @pl.loop(0, 2)
        def _(h):
            p, nxt, prv = place(h)
            k = step - 3 * p

            @pl.when((p > 0) & (k >= 0) & (k < K))
            def _():
                chain_copy(h, k, prv).wait_recv()

                @pl.when(p < S - 1)
                def _():
                    part_v[h, k] = (part_v[h, k].astype(F32) + part_recv[h, k].astype(F32)).astype(BF16)
                    chain_copy(h, k, nxt).start()

                @pl.when(p == S - 1)
                def _():
                    first = part_v[h, k, 0].astype(F32) + part_recv[h, k, 0].astype(F32)
                    second = part_v[h, k, 1].astype(F32) + part_recv[h, k, 1].astype(F32)
                    hidden_v[chunk(h, k), :] = (first / (1.0 + jnp.exp(-first)) * second).astype(BF16)
                    back_copy(h, k, prv).start()
                    finish(h, k)

            q = step - 3 * (S - 1) - 3 * (S - 1 - p)

            @pl.when((p < S - 1) & (q >= 0) & (q < K))
            def _():
                back_copy(h, q, nxt).wait_recv()

                @pl.when(p > 0)
                def _():
                    back_copy(h, q, prv).start()

                finish(h, q)

    acc_v[...] += term_send[group(l), :].astype(F32)

    def add_term(t):
        list_recv(TERMS, t, term_send.at[group(t)], term_recv.at[t])
        acc_v[...] += term_recv[t].astype(F32)

    others(L, l, add_term)
    stream = acc_v[...]
    square_v[s] = jnp.broadcast_to(jnp.sum(stream * stream, axis=1, keepdims=True), (G, 128))
    others(S, s, lambda t: shard_copy(SQUARES, t, square_v.at[s], square_v.at[s]).start())

    for j in (3, 4):
        locals_[j].wait()

    def recv_small(t):
        list_recv(IDX2, t, idx_v.at[l], idx_v.at[t])
        list_recv(CENT, t, cents.at[:, cols(s)], cent_v.at[t])

    others(L, l, recv_small)
    mine_idx = idx_v[l].reshape(G, 256)
    ids, alive = mine_idx[:, :1], mine_idx[:, 128:129].astype(F32)
    coarse = jnp.zeros((G, C), F32)
    for g in range(L):
        for k in range(own):
            row = cent_v[g, k:k + 1, :].astype(BF16).astype(F32)
            coarse = coarse + jnp.where(ids == g * own + k, row, 0.0)
    every = idx_v[...].reshape(N, 256)
    counts = [
        jnp.sum(
            jnp.where(every[:, :128] == l * own + k, every[:, 128:].astype(F32), 0.0),
            axis=0, keepdims=True,
        )[:, :1]
        for k in range(own)
    ]

    others(S, s, lambda t: shard_recv(SQUARES, t, square_v.at[s], square_v.at[t]))
    squares = square_v[0]
    for j in range(1, S):
        squares = squares + square_v[j]
    scale = lax.rsqrt(squares[:, :1] / D + 1e-05)
    embedding = (acc_v[...] * scale * gain_v[...]).astype(BF16).astype(F32)
    weighted = alive * embedding
    for g in range(L):
        for k in range(own):
            sum_send[g, k:k + 1, :] = jnp.sum(
                jnp.where(ids == g * own + k, weighted, 0.0), axis=0, keepdims=True
            )
    others(L, l, lambda t: list_copy(SUMS, t, sum_send.at[t], sum_recv.at[l]).start())
    res_send[...] = (alive * (embedding - coarse)).reshape(S, R, C).astype(BF16)
    others(S, s, lambda t: shard_copy(RESID, t, res_send.at[t], res_recv.at[s]).start())
    res_recv[s] = res_send[s]
    sum_recv[l] = sum_send[l]
    others(L, l, lambda t: list_recv(SUMS, t, sum_send.at[t], sum_recv.at[t]))
    for k in range(own):
        total = cent_v[l, k:k + 1, :]
        for g in range(L):
            total = total + sum_recv[g, k:k + 1, :]
        fresh_v[s, k:k + 1, :] = total / (1.0 + counts[k])
    others(S, s, lambda t: shard_copy(FRESH, t, fresh_v.at[s], fresh_v.at[s]).start())
    others(S, s, lambda t: shard_recv(RESID, t, res_send.at[t], res_recv.at[t]))
    for j in range(S):
        out_res[:, j * C:(j + 1) * C] = res_recv[j]
    others(S, s, lambda t: shard_recv(FRESH, t, fresh_v.at[s], fresh_v.at[t]))
    for j in range(S):
        out_fresh[:, j * C:(j + 1) * C] = fresh_v[j]

    def shard_sent(t):
        shard_copy(FEAT, t, feat.at[:, cols(t)], group_v.at[s]).wait_send()
        shard_copy(IDX, t, idx, idx_v.at[l, s]).wait_send()
        shard_copy(SQUARES, t, square_v.at[s], square_v.at[s]).wait_send()
        shard_copy(RESID, t, res_send.at[t], res_recv.at[s]).wait_send()
        shard_copy(FRESH, t, fresh_v.at[s], fresh_v.at[s]).wait_send()

    others(S, s, shard_sent)

    def list_sent(t):
        list_copy(IDX2, t, idx_v.at[l], idx_v.at[l]).wait_send()
        list_copy(CENT, t, cents.at[:, cols(s)], cent_v.at[l]).wait_send()
        list_copy(TERMS, t, term_send.at[group(t)], term_recv.at[l]).wait_send()
        list_copy(SUMS, t, sum_send.at[t], sum_recv.at[l]).wait_send()

    others(L, l, list_sent)

    def rows_sent(t):
        list_copy(ROWS, t, rows_v.at[group(l)], rows_v.at[group(l)]).wait_send()

    peers(l, rows_sent)
    rows_sent(mate)
    peers(l, lambda t: pass_on(t).wait_send())

    @pl.loop(0, 2)
    def _(h):
        p, nxt, prv = place(h)

        @pl.loop(0, K)
        def _(k):
            @pl.when(p < S - 1)
            def _():
                chain_copy(h, k, nxt).wait_send()

            @pl.when(p > 0)
            def _():
                back_copy(h, k, prv).wait_send()


def solution(mesh):
    L, S = mesh.shape["list"], mesh.shape["shard"]

    def body(features, norm_gain, gate_weight, up_weight, down_weight, centroids, list_ids, live):
        R, D = features.shape
        C, F = gate_weight.shape
        own = centroids.shape[0]
        G, N = R * S, R * S * L
        lane = lax.broadcasted_iota(jnp.int32, (R, 256), 1)
        packed = jnp.where(lane < 128, list_ids[:, None], live[:, None])
        return pl.pallas_call(
            functools.partial(kernel, L, S),
            out_shape=(
                jax.ShapeDtypeStruct((R, D), BF16),
                jax.ShapeDtypeStruct((own, D), F32),
            ),
            in_specs=[pl.BlockSpec(memory_space=pl.ANY)] * 7,
            out_specs=[pl.BlockSpec(memory_space=pltpu.VMEM)] * 2,
            scratch_shapes=[
                pltpu.VMEM((F, C), BF16),
                pltpu.VMEM((F, C), BF16),
                pltpu.VMEM((F, C), BF16),
                pltpu.VMEM((1, C), F32),
                pltpu.VMEM((L, own, C), F32),
                pltpu.VMEM((L, S, R, 256), jnp.int32),
                pltpu.VMEM((S, R, C), BF16),
                pltpu.VMEM((N, C), BF16),
                pltpu.VMEM((2, L, 2, G // 2, F), BF16),
                pltpu.VMEM((2, L, 2, G // 2, F), BF16),
                pltpu.VMEM((N, F), BF16),
                pltpu.VMEM((N, C), BF16),
                pltpu.VMEM((L, G, C), BF16),
                pltpu.VMEM((G, C), F32),
                pltpu.VMEM((S, G, 128), F32),
                pltpu.VMEM((S, R, C), BF16),
                pltpu.VMEM((S, R, C), BF16),
                pltpu.VMEM((L, own, C), F32),
                pltpu.VMEM((L, own, C), F32),
                pltpu.VMEM((S, own, C), F32),
                pltpu.SemaphoreType.DMA((7,)),
                pltpu.SemaphoreType.DMA((5, S)),
                pltpu.SemaphoreType.DMA((5, S)),
                pltpu.SemaphoreType.DMA((6, L)),
                pltpu.SemaphoreType.DMA((6, L)),
                pltpu.SemaphoreType.DMA((2, L)),
                pltpu.SemaphoreType.DMA((2, L)),
                pltpu.SemaphoreType.DMA((2, L)),
                pltpu.SemaphoreType.DMA((2, L)),
            ],
            compiler_params=pltpu.CompilerParams(collective_id=0, has_side_effects=True),
        )(features, norm_gain, gate_weight.T, up_weight.T, down_weight, centroids, packed)

    in_specs = (
        P(("list", "shard"), None),
        P(),
        P("shard", "list"),
        P("shard", "list"),
        P("list", "shard"),
        P("list", None),
        P(("list", "shard")),
        P(("list", "shard")),
    )
    out_specs = (P(("list", "shard"), None), P("list", None))
    return jax.shard_map(body, mesh=mesh, in_specs=in_specs, out_specs=out_specs, check_vma=False)
```
